32 devices in a mesh: parts: 2 (over x), ctx: 8 (over z, y), head: 2 (over core).
Axes of the slice: x: 2, y: 2, z: 4, core: 2. Of those that a mesh axis runs over, the one named last changes fastest.
Arguments:
- channels: bfloat16 [2048, 2048], P(('parts', 'ctx'), 'head'), parts along dimension 0, may hold values from -6 to 6
- gate_channels: bfloat16 [2048, 2048], P(('parts', 'ctx'), 'head'), parts along dimension 0, may hold values from -6 to 6
- bmat: bfloat16 [2048, 512], P(('parts', 'ctx'), 'head'), parts along dimension 0, may hold values from -4 to 4
- cmat: bfloat16 [2048, 512], P(('parts', 'ctx'), 'head'), parts along dimension 0, may hold values from -4 to 4
- dt: float32 [2048, 32], P(('parts', 'ctx'), 'head'), parts along dimension 0, may hold values from 0.1 to 40
- rates: float32 [32], P('head'), may hold values from 0.00029296876 to 0.03
- skip: float32 [32], P('head'), may hold values from 0.5 to 2
- norm_gain: float32 [2048], P('head'), may hold values from 0.25 to 1.75
- docs: int32 [2048], P(('parts', 'ctx')), parts along dimension 0, may hold values from 0 to 3, never falling along the last dimension, each value on 1 to 512 neighbouring positions
- w_out: bfloat16 [2048, 2688], P('head', 'ctx'), may hold values from -0.125 to 0.125
- residual: bfloat16 [2048, 2688], P(('parts', 'ctx', 'head')), parts along dimension 0, may hold values from -6 to 6
- moe_gain: float32 [2688], replicated, may hold values from 0.25 to 1.75
- experts: int32 [2048, 6], P(('parts', 'ctx', 'head')), parts along dimension 0, may hold values from 0 to 15, all different within a row; in each aligned block of 64 rows (0 to 63, 64 to 127, ...) at most 36 rows name the same one
- gates: float32 [2048, 6], P(('parts', 'ctx', 'head')), parts along dimension 0, may hold values from 0.05 to 0.5
- w_up: bfloat16 [16, 2688, 928], P(('ctx', 'head')), may hold values from -0.125 to 0.125
- w_down: bfloat16 [16, 928, 2688], P(('ctx', 'head')), may hold values from -0.1875 to 0.1875
Outputs:
- layer_out: bfloat16 [2048, 2688], P(('parts', 'ctx', 'head')), parts along dimension 0
The draws below stay inside these ranges and needn't reach their ends.
There are 2 independent parts, one for each index of `parts`. The reference program is written for one: setup_inputs(seed, part) draws one part's arguments, and reference() takes and returns one part's arrays. A program takes and returns all parts, laid end to end along the dimension named above; an argument that names none is the same for every part. Nothing has to cross between parts.
Inputs may be any that keep to these rules, and one draw needn't show every extreme that they name: Each row names 6 different experts; in each aligned block of 64 rows (the rows of one device) no expert is named by more than 36 rows. `docs`: ids never fall along the tokens; a document starts where the id changes and holds at most half of the 1024 tokens.
All inputs are finite; a program needn't handle non-finite values.
Results may differ from the reference program's by a relative error of at most 0.013.
Values may be sent and summed in bfloat16 or wider, within the bound.
No kernel may reach another device: no remote copies, remote signals or barrier semaphores. Data moves between devices by JAX's collectives and lax.ppermute only.
A program may use at most 128 MiB of HBM per device.

```python
import math
import jax
import jax.numpy as jnp
import numpy as np
from jax import lax

D = 2688
HEADS = 32
HEAD_DIM = 64
GROUPS = 4
STATE = 128
FF = 928
TOP = 6
TOKENS = 1024
ROWS_DEV = 64
EXPERTS = 16
CAP = 36
N_CTX = 8


def draw_dt(key, part):
    key = jax.random.fold_in(key, 11)
    first, second, third = jax.random.split(key, 3)
    level = jax.random.uniform(first, (TOKENS, HEADS), jnp.float32, -0.8, 0.8)
    rough = jnp.exp(level)
    spots = jax.random.randint(second, (8,), 0, TOKENS)
    height = jax.random.uniform(third, (8,), jnp.float32, 10.0, 40.0)
    lifted = jnp.zeros((TOKENS,), jnp.float32).at[spots].max(height)
    return jnp.maximum(rough, lifted[:, None])


def steps_of(stream_key, dims, pieces, smallest, top_value):
    level = 1.0
    for position, blocks in pieces:
        draws = jax.random.uniform(jax.random.fold_in(jax.random.fold_in(stream_key, 6), position), (blocks,), jnp.float32, smallest / len(pieces), top_value / len(pieces))
        level = level * jnp.repeat(jnp.exp(draws), dims[position] // blocks).reshape((-1,) + (1,) * (len(dims) - 1 - position))
    return level


def profile(amount, total, limit, lean):
    portions = [(1 << 20) // math.isqrt(rank ** lean) + 1 for rank in range(2, amount + 1)]
    spare, given = total - limit - (amount - 1), [1] * (amount - 1)
    while spare > 0:
        candidates = [i for i in range(amount - 1) if given[i] < limit]
        whole, budget = sum([portions[i] for i in candidates]), spare
        for i in candidates:
            addition = min(limit - given[i], max(1, budget * portions[i] // whole), spare)
            given[i] = given[i] + addition
            spare = spare - addition
    return np.array([limit] + given)


def uneven_parts(stream_key, amount, total, limit, skew):
    if amount == 2:
        one = jax.random.randint(stream_key, (), max(1, total - limit), min(limit, total - 1) + 1)
        return jnp.stack([one, total - one])
    sizes = jnp.asarray(profile(amount, total, limit, skew), jnp.int32)
    pairs = (amount - 1) // 2
    source_of, sink = sizes[1:1 + 2 * pairs:2], sizes[2:2 + 2 * pairs:2]
    margin = jnp.minimum(source_of - 1, limit - sink)
    shifted = jax.random.randint(jax.random.fold_in(stream_key, 1), (pairs,), 0, 1 << 20) % (margin + 1)
    sizes = sizes.at[1:1 + 2 * pairs:2].set(source_of - shifted).at[2:2 + 2 * pairs:2].set(sink + shifted)
    return sizes[jax.random.permutation(jax.random.fold_in(stream_key, 2), amount)]


def deal_out(rng, own, number, rows, number_of, top, most, lean):
    order = jax.random.permutation(rng, number_of)
    packed, usual = portions_of(number_of, rows * top, most, lean, True), portions_of(number_of, rows * top, most, lean, False)
    places = jnp.arange(number_of)

    def named(lengths, turn):
        used = int((lengths > 0).sum())
        fixed = max(1, used // 4)
        shifted = fixed + (places - fixed + turn * (used - fixed)) % max(1, number_of - fixed)
        return jnp.zeros((number_of,), jnp.int32).at[order[jnp.where(places < fixed, places, shifted)]].set(jnp.asarray(lengths, jnp.int32))

    lengths = jnp.where(number % 4 == 0, named(packed, number // 4), named(usual, number - number // 4 - 1))
    mixed = jax.random.permutation(jax.random.fold_in(own, 3), number_of)
    donor, receiver = mixed[0:number_of // 2 * 2:2], mixed[1:number_of // 2 * 2:2]
    margin = jnp.minimum(lengths[donor] - 1, most - lengths[receiver]) // 2
    margin = jnp.where((donor == order[0]) | (receiver == order[0]) | (lengths[receiver] == 0), 0, jnp.maximum(margin, 0))
    shifted = jax.random.randint(jax.random.fold_in(own, 4), (number_of // 2,), 0, 1 << 20) % (margin + 1)
    lengths = lengths.at[donor].add(-shifted).at[receiver].add(shifted)
    items = jnp.searchsorted(jnp.cumsum(lengths), jnp.arange(rows * top), side="right").astype(jnp.int32)
    listing = items.reshape(top, rows).T
    listing = listing[jax.random.permutation(jax.random.fold_in(own, 1), rows)]
    turn = jax.random.randint(jax.random.fold_in(own, 2), (rows, 1), 0, top)
    return jnp.take_along_axis(listing, (jnp.arange(top)[None, :] + turn) % top, axis=1)


def portions_of(number_of, total, reach, slope, full):
    loads = [(1 << 20) // math.isqrt(grade ** slope) + 1 for grade in range(1, number_of + 1)]
    largest = reach if full else min(reach, max(-(-total // number_of), total * loads[0] // sum(loads)))
    least = 1 if total - largest >= number_of - 1 else 0
    holding, surplus = [largest] + [least] * (number_of - 1), total - largest - least * (number_of - 1)
    while surplus > 0:
        movable = [i for i in range(1, number_of) if holding[i] < largest] or [i for i in range(1, number_of) if holding[i] < reach]
        pool, remaining = sum([loads[i] for i in movable]), surplus
        for i in movable:
            more = min(reach - holding[i], max(1, remaining * loads[i] // pool), surplus)
            holding[i] = holding[i] + more
            surplus = surplus - more
    return np.array(holding)


def gaussian(stream_key, dims, scale, bound, cuts=(), kind=jnp.bfloat16):
    level = steps_of(stream_key, dims, cuts, -0.22, 0.18) if cuts else 1.0
    result = jax.random.normal(stream_key, dims, jnp.float32) * scale * level
    return jnp.minimum(jnp.maximum(result, -bound), bound).astype(kind)


def setup_inputs(seed: int = 0, part: int = 0) -> dict:
    arg_keys = jax.random.split(jax.random.key(seed), 17)
    own_keys = jax.random.split(jax.random.fold_in(arg_keys[16], part), 17)
    channels = gaussian(own_keys[0], (TOKENS, HEADS * HEAD_DIM), 1.0, 6.0, ((0, 8), (1, 2)))
    gate_channels = gaussian(own_keys[1], (TOKENS, HEADS * HEAD_DIM), 1.0, 6.0, ((0, 8), (1, 2)))
    bmat = gaussian(own_keys[2], (TOKENS, GROUPS * STATE), (STATE ** -0.25), 4.0, ((0, 8), (1, 2)))
    cmat = gaussian(own_keys[3], (TOKENS, GROUPS * STATE), (STATE ** -0.25), 4.0, ((0, 8), (1, 2)))
    dt = draw_dt(jax.random.fold_in(jax.random.fold_in(arg_keys[16], part), 71), part)
    rates = jnp.clip(jnp.exp(math.log(0.03) - 4.6288867 * jax.random.uniform(arg_keys[5], (HEADS,), jnp.float32) ** steps_of(arg_keys[5], (HEADS,), ((0, 2),), -0.2, 0.2)), 0.00029296876, 0.03)
    skip = jnp.clip(0.5 + 1.5 * jax.random.uniform(arg_keys[6], (HEADS,), jnp.float32) ** steps_of(arg_keys[6], (HEADS,), ((0, 2),), -0.2, 0.2), 0.5, 2.0)
    norm_gain = jnp.clip(1.0 + 0.15 * jax.random.normal(arg_keys[7], (HEADS * HEAD_DIM,), jnp.float32), 0.25, 1.75)
    docs = jnp.searchsorted(jnp.cumsum(uneven_parts(own_keys[8], max(4, N_CTX // 4), TOKENS, TOKENS // 2, 2)), jnp.arange(TOKENS), side="right").astype(jnp.int32)
    w_out = gaussian(arg_keys[9], (HEADS * HEAD_DIM, D), (HEADS * HEAD_DIM) ** -0.5, 0.125, ((0, 2), (1, 8)))
    residual = gaussian(own_keys[10], (TOKENS, D), 1.0, 6.0, ((0, 16),))
    moe_gain = jnp.clip(1.0 + 0.15 * jax.random.normal(arg_keys[11], (D,), jnp.float32), 0.25, 1.75)
    experts_keys = jax.random.split(jax.random.fold_in(own_keys[12], 1), TOKENS // ROWS_DEV)
    experts_turns = jax.random.permutation(jax.random.fold_in(own_keys[12], 3), TOKENS // ROWS_DEV)
    experts = jax.vmap(lambda own, number: deal_out(jax.random.fold_in(own_keys[12], 2), own, number, ROWS_DEV, EXPERTS, TOP, CAP, 2))(experts_keys, experts_turns).reshape((TOKENS, TOP))
    gates = jnp.clip(jnp.exp(math.log(0.5) - 2.3025851 * jax.random.uniform(own_keys[13], (TOKENS, TOP), jnp.float32) ** steps_of(own_keys[13], (TOKENS, TOP), ((0, 16),), -0.2, 0.2)), 0.05, 0.5)
    w_up = gaussian(arg_keys[14], (EXPERTS, D, FF), D ** -0.5, 0.125, ((0, 16),))
    w_down = gaussian(arg_keys[15], (EXPERTS, FF, D), FF ** -0.5, 0.1875, ((0, 16),))
    return dict(channels=channels, gate_channels=gate_channels, bmat=bmat, cmat=cmat, dt=dt, rates=rates, skip=skip, norm_gain=norm_gain, docs=docs, w_out=w_out, residual=residual, moe_gain=moe_gain, experts=experts, gates=gates, w_up=w_up, w_down=w_down)


EPS = 1e-05
BLOCK_ROWS = 128

def silu(value):
    return value / (1.0 + jnp.exp(-value))

def mamba_scan(channels, bmat, cmat, dt, rates, skip, docs):
    heads = rates.shape[0]
    per_group = heads // GROUPS
    xs = channels.astype(jnp.float32).reshape(TOKENS, heads, HEAD_DIM)
    bs = bmat.astype(jnp.float32).reshape(TOKENS, GROUPS, STATE)
    cs = cmat.astype(jnp.float32).reshape(TOKENS, GROUPS, STATE)
    before = jnp.concatenate([docs[:1] - 1, docs[:-1]])
    keep = (docs == before).astype(jnp.float32)

    def step(state, inputs):
        x_now, b_now, c_now, dt_now, keep_now = inputs
        decay = jnp.exp(-rates * dt_now) * keep_now
        b_heads = jnp.repeat(b_now, per_group, axis=0)
        c_heads = jnp.repeat(c_now, per_group, axis=0)
        state = decay[:, None, None] * state + (dt_now[:, None] * x_now)[:, :, None] * b_heads[:, None, :]
        y_now = lax.optimization_barrier(jnp.sum(state * c_heads[:, None, :], axis=2)) + skip[:, None] * x_now
        return (state, y_now)
    start = jnp.zeros((heads, HEAD_DIM, STATE), jnp.float32)
    _, ys = lax.scan(step, start, (xs, bs, cs, dt, keep))
    return ys.reshape(TOKENS, heads * HEAD_DIM)

def gated_norm(scan, gate_channels, gain):
    gated = scan * silu(gate_channels.astype(jnp.float32))
    width = HEADS * HEAD_DIM // GROUPS
    grouped = gated.reshape(gated.shape[0], -1, width)
    square = lax.optimization_barrier(jnp.mean(grouped * grouped, axis=2, keepdims=True))
    normed = grouped / jnp.sqrt(square + EPS)
    return normed.reshape(gated.shape[0], -1) * gain

def experts_apply(moe_in, experts, gates, w_up, w_down):
    picks = TOKENS * TOP
    flat = experts.reshape(-1).astype(jnp.int32)
    order = jnp.argsort(flat, stable=True).astype(jnp.int32)
    labels = jnp.arange(EXPERTS, dtype=jnp.int32)
    counts = lax.optimization_barrier(jnp.sum((flat[None, :] == labels[:, None]).astype(jnp.int32), axis=1)).astype(jnp.int32)
    starts = (jnp.cumsum(counts) - counts).astype(jnp.int32)
    blocks = ((counts + BLOCK_ROWS - 1) // BLOCK_ROWS).astype(jnp.int32)
    block_ends = jnp.cumsum(blocks).astype(jnp.int32)
    block_starts = (block_ends - blocks).astype(jnp.int32)
    nblocks = picks // BLOCK_ROWS + EXPERTS
    sorted_experts = flat[order]
    rank = jnp.arange(picks, dtype=jnp.int32) - starts[sorted_experts]
    padded = (block_starts[sorted_experts] * BLOCK_ROWS + rank).astype(jnp.int32)
    source_row = jnp.full((nblocks * BLOCK_ROWS,), TOKENS, jnp.int32).at[padded].set(order // TOP)
    block_ids = jnp.arange(nblocks, dtype=jnp.int32)
    owner = lax.optimization_barrier(jnp.sum((block_ends[None, :] <= block_ids[:, None]).astype(jnp.int32), axis=1))
    owner = jnp.minimum(owner, EXPERTS - 1).astype(jnp.int32)
    table = jnp.concatenate([moe_in, jnp.zeros((1, D), jnp.bfloat16)], axis=0)

    def one_block(inputs):
        rows_index, expert = inputs
        rows = table[rows_index].astype(jnp.float32)
        up = jnp.dot(rows, w_up[expert].astype(jnp.float32), preferred_element_type=jnp.float32)
        act = jnp.square(jnp.maximum(up, 0.0)).astype(jnp.bfloat16)
        down = jnp.dot(act.astype(jnp.float32), w_down[expert].astype(jnp.float32), preferred_element_type=jnp.float32)
        return down.astype(jnp.bfloat16)
    results = lax.map(one_block, (source_row.reshape(nblocks, BLOCK_ROWS), owner)).reshape(-1, D)
    pick_pos = jnp.zeros((picks,), jnp.int32).at[order].set(padded)
    chosen = results[pick_pos].reshape(TOKENS, TOP, D).astype(jnp.float32)
    return lax.optimization_barrier(jnp.sum(chosen * gates[:, :, None], axis=1))

def reference(channels, gate_channels, bmat, cmat, dt, rates, skip, norm_gain, docs, w_out, residual, moe_gain, experts, gates, w_up, w_down):
    scan = mamba_scan(channels, bmat, cmat, dt, rates, skip, docs)
    normed_scan = gated_norm(scan, gate_channels, norm_gain).astype(jnp.bfloat16)
    mamba_out = jnp.dot(normed_scan, w_out, preferred_element_type=jnp.float32)
    hidden = (residual.astype(jnp.float32) + mamba_out).astype(jnp.bfloat16)
    widened = hidden.astype(jnp.float32)
    moe_in = (widened / jnp.sqrt(lax.optimization_barrier(jnp.mean(widened * widened, axis=1, keepdims=True)) + EPS) * moe_gain).astype(jnp.bfloat16)
    mixture = experts_apply(moe_in, experts, gates, w_up, w_down)
    return (widened + mixture).astype(jnp.bfloat16)
```

```python
import functools

import jax
import jax.numpy as jnp
from jax import lax
from jax.experimental import pallas as pl
from jax.experimental.pallas import tpu as pltpu
from jax.sharding import PartitionSpec as P

HEADS = 32
HEAD_DIM = 64
GROUPS = 4
STATE = 128


EPS = 1e-05


def entering(array, axis, combine, identity):
    size, place = (lax.axis_size(axis), lax.axis_index(axis))
    everything = jax.tree.map(lambda part: lax.all_gather(part, axis), array)
    start = jax.tree.map(
        lambda part, zero: jnp.broadcast_to(jnp.asarray(zero, part.dtype), part.shape),
        array,
        identity,
    )

    def lap(k, before):
        reached = k < place
        new = combine(before, jax.tree.map(lambda part: part[k], everything))
        return jax.tree.map(lambda a, b: jnp.where(reached, a, b), new, before)

    return lax.fori_loop(0, size, lap, start)


def silu(value):
    return value / (1.0 + jnp.exp(-value))


def combine_states(earlier, later):
    first_a, last_a, decay_a, state_a = earlier
    first_b, last_b, decay_b, state_b = later
    linked = ((last_a == first_b) | (last_a < 0) | (first_b < 0)).astype(jnp.float32)
    carried = decay_b * linked
    decay = carried * decay_a
    state = state_b + carried[:, None, None] * state_a
    first = jnp.where(first_a < 0, first_b, first_a)
    last = jnp.where(last_b < 0, last_a, last_b)
    return (first, last, decay, state)


def group_terms(inputs, causal, ending):
    x_group, b_group, c_group, log_group, dt_group = inputs
    scores = jnp.dot(c_group, b_group.T, preferred_element_type=jnp.float32)
    gap = jnp.where(causal[:, :, None], log_group[:, None, :] - log_group[None, :, :], -jnp.inf)
    weight = jnp.exp(gap) * scores[:, :, None] * dt_group[None, :, :]
    inner = jnp.einsum("tsh,shp->thp", weight, x_group, precision=lax.Precision.HIGHEST)
    tail = jnp.exp(log_group[-1][None, :] - log_group) * ending[:, None] * dt_group
    end_state = jnp.einsum(
        "sh,shp,sn->hpn",
        tail,
        x_group,
        b_group.astype(jnp.float32),
        precision=lax.Precision.HIGHEST,
    )
    return (inner, end_state)


def expert_rows(received, up_weight, down_weight):
    sources, items, width = received.shape
    rows = received.reshape(sources * items, width)
    up = jnp.dot(rows, up_weight, preferred_element_type=jnp.float32)
    act = jnp.square(jnp.maximum(up, 0.0)).astype(jnp.bfloat16)
    result = jnp.dot(act, down_weight, preferred_element_type=jnp.float32).astype(jnp.bfloat16)
    return result.reshape(sources, items, width)


LANES = 128


def dot(left, right, left_dim, right_dim):
    return lax.dot_general(
        left,
        right,
        (((left_dim,), (right_dim,)), ((), ())),
        preferred_element_type=jnp.float32,
    )


def whole_spec():
    return pl.BlockSpec(memory_space=pltpu.VMEM)


def scalar_spec():
    return pl.BlockSpec(memory_space=pltpu.SMEM)


def call(kernel, outs, specs, cost, limit, name):
    return pl.pallas_call(
        kernel,
        in_specs=specs,
        out_specs=[whole_spec() for _ in outs],
        out_shape=outs,
        compiler_params=pltpu.CompilerParams(vmem_limit_bytes=limit << 20),
        cost_estimate=pl.CostEstimate(flops=cost[0], bytes_accessed=cost[1], transcendentals=0),
        name=name,
    )


def shaped(shape, dtype):
    return jax.ShapeDtypeStruct(shape, dtype)


def three_pieces(value):
    first = value.astype(jnp.bfloat16)
    rest = value - first.astype(jnp.float32)
    second = rest.astype(jnp.bfloat16)
    third = (rest - second.astype(jnp.float32)).astype(jnp.bfloat16)
    return (first, second, third)


def packed_width(experts_all):
    return -(-3 * experts_all // LANES) * LANES


def moe_rows_kernel(experts_all, mixed, residual, gain, experts, gates, hidden_out, packed_out):
    rows, width = residual.shape
    hidden = (residual[...].astype(jnp.float32) + mixed[...].astype(jnp.float32)).astype(jnp.bfloat16)
    hidden_out[...] = hidden
    wide = hidden.astype(jnp.float32)
    scale = jnp.sqrt(jnp.mean(wide * wide, axis=1, keepdims=True) + EPS)
    packed_out[:, :width] = (wide / scale * gain[...]).astype(jnp.bfloat16)
    lanes = packed_out.shape[1] - width
    lane = lax.broadcasted_iota(jnp.int32, (rows, lanes), 1)
    table = jnp.zeros((rows, lanes), jnp.float32)
    for k in range(experts.shape[1]):
        chosen = experts[:, k : k + 1]
        hit = (lane == chosen) | (lane == chosen + experts_all) | (lane == chosen + 2 * experts_all)
        table = table + jnp.where(hit, gates[:, k : k + 1], 0.0)
    first, second, third = three_pieces(table)
    picked = jnp.where(lane < experts_all, first, jnp.where(lane < 2 * experts_all, second, third))
    packed_out[:, width:] = picked


def expert_pair_kernel(experts_all, ids, near, far, up0, down0, up1, down1, near_out, far_out):
    rows = near.shape[0]
    width = near_out.shape[1]
    x = jnp.concatenate([near[:, :width], far[:, :width]], axis=0)
    table = jnp.concatenate([near[:, width:], far[:, width:]], axis=0).astype(jnp.float32)
    lane = lax.broadcasted_iota(jnp.int32, table.shape, 1)
    acts, weights = ([], [])
    for k, up in enumerate((up0, up1)):
        value = dot(x, up[...], 1, 1)
        acts.append(jnp.square(jnp.maximum(value, 0.0)).astype(jnp.bfloat16))
        mine = ids[k]
        hit = (lane == mine) | (lane == mine + experts_all) | (lane == mine + 2 * experts_all)
        weights.append(jnp.sum(jnp.where(hit, table, 0.0), axis=1, keepdims=True))
    step = width
    for part in (3, 2):
        if width % (part * LANES) == 0:
            step = width // part
            break
    for at in range(0, width, step):
        piece = pl.ds(at, step)
        result = dot(acts[0], down0[:, piece], 1, 0) * weights[0] + dot(acts[1], down1[:, piece], 1, 0) * weights[1]
        near_out[:, piece] = result[:rows].astype(near_out.dtype)
        far_out[:, piece] = result[rows:].astype(far_out.dtype)


def moe_by_sums(mixed, residual, moe_gain, experts, gates, w_up, w_down):
    rows, width = residual.shape
    units = w_down.shape[1]
    ctx_count, head_count = (lax.axis_size("ctx"), lax.axis_size("head"))
    experts_all = ctx_count * head_count
    high = ctx_count // 2
    ring = [(z * 2 + y, (z + 1) % high * 2 + y) for z in range(high) for y in range(2)]
    across = [(z * 2 + y, z * 2 + 1 - y) for z in range(high) for y in range(2)]
    swap = [(0, 1), (1, 0)]
    up_own = jnp.swapaxes(w_up[0], 0, 1)
    down_own = w_down[0]
    up_other = lax.ppermute(up_own, "head", swap)
    down_other = lax.ppermute(down_own, "head", swap)
    mine = lax.axis_index("ctx") * head_count + lax.axis_index("head")
    other = lax.axis_index("ctx") * head_count + 1 - lax.axis_index("head")
    ids = jnp.stack([mine, other]).astype(jnp.int32)
    extra = packed_width(experts_all)
    hidden, packed = call(
        functools.partial(moe_rows_kernel, experts_all),
        [shaped((rows, width), jnp.bfloat16), shaped((rows, width + extra), jnp.bfloat16)],
        [whole_spec()] * 5,
        (10 * rows * width, 8 * rows * width),
        8,
        "moe_rows",
    )(mixed, residual, moe_gain.reshape(1, width), experts, gates)
    near = [packed]
    for _ in range(1, high):
        near.append(lax.ppermute(near[-1], "ctx", ring))
    far = [lax.ppermute(value, "ctx", across) for value in near]
    partials = []
    for r in range(high):
        partials.append(
            call(
                functools.partial(expert_pair_kernel, experts_all),
                [shaped((rows, width), jnp.bfloat16)] * 2,
                [scalar_spec()] + [whole_spec()] * 6,
                (16 * rows * width * units, 8 * width * units),
                26,
                "expert_pair",
            )(ids, near[r], far[r], up_own, down_own, up_other, down_other)
        )
    sums = [
        own.astype(jnp.float32) + lax.ppermute(away, "ctx", across).astype(jnp.float32)
        for own, away in partials
    ]
    total = None
    for r in list(range(1, high)) + [0]:
        value = sums[r] if total is None else sums[r] + total.astype(jnp.float32)
        if r == 0:
            return (hidden.astype(jnp.float32) + value).astype(jnp.bfloat16)
        total = lax.ppermute(value.astype(jnp.bfloat16), "ctx", ring)


def slots_of(rows, top, experts_all):
    return min(rows, max(4, 3 * rows * top // (2 * experts_all)))


def moe_by_rows(mixed, residual, moe_gain, experts, gates, w_up, w_down):
    mamba_out = mixed.astype(jnp.float32)
    hidden = (residual.astype(jnp.float32) + mamba_out).astype(jnp.bfloat16)
    widened = hidden.astype(jnp.float32)
    moe_in = (
        widened / jnp.sqrt(jnp.mean(widened * widened, axis=1, keepdims=True) + EPS) * moe_gain
    ).astype(jnp.bfloat16)
    rows_dev = moe_in.shape[0]
    top = experts.shape[1]
    width = moe_in.shape[1]
    ctx_count = lax.axis_size("ctx")
    head_count = lax.axis_size("head")
    experts_all = ctx_count * head_count
    capacity = slots_of(rows_dev, top, experts_all)
    picks = experts.reshape(-1)
    pick_index = jnp.arange(picks.shape[0], dtype=jnp.int32)
    earlier = (picks[:, None] == picks[None, :]) & (pick_index[None, :] < pick_index[:, None])
    slot = jnp.sum(earlier.astype(jnp.int32), axis=1)
    target = (picks * capacity + slot).reshape(rows_dev, top)
    places = jnp.arange(experts_all * capacity, dtype=jnp.int32)
    routing = jnp.any(target[None, :, :] == places[:, None, None], axis=2).astype(jnp.bfloat16)
    outgoing = jnp.dot(routing, moe_in, preferred_element_type=jnp.float32).astype(jnp.bfloat16)
    outgoing = outgoing.reshape(experts_all, capacity, width)
    up_weight = w_up[0]
    down_weight = w_down[0]
    results = expert_rows(
        lax.all_to_all(outgoing, ("ctx", "head"), split_axis=0, concat_axis=0, tiled=True),
        up_weight,
        down_weight,
    )
    returned = lax.all_to_all(results, ("ctx", "head"), split_axis=0, concat_axis=0, tiled=True)
    flat_back = returned.reshape(experts_all * capacity, width)
    chosen = flat_back[target].astype(jnp.float32)
    mixture = jnp.sum(chosen * gates[:, :, None], axis=1)
    return (widened + mixture).astype(jnp.bfloat16)


def local(
    channels,
    gate_channels,
    bmat,
    cmat,
    dt,
    rates,
    skip,
    norm_gain,
    docs,
    w_out,
    residual,
    moe_gain,
    experts,
    gates,
    w_up,
    w_down,
):
    length = channels.shape[0]
    heads = dt.shape[1]
    groups = bmat.shape[1] // STATE
    per_group = heads // groups
    logs = jnp.cumsum(-rates[None, :] * dt, axis=0)
    x_wide = channels.astype(jnp.float32).reshape(length, groups, per_group, HEAD_DIM)
    b_split = bmat.reshape(length, groups, STATE)
    c_split = cmat.reshape(length, groups, STATE)
    position = jnp.arange(length, dtype=jnp.int32)
    causal = (docs[:, None] == docs[None, :]) & (position[:, None] >= position[None, :])
    ending = (docs == docs[length - 1]).astype(jnp.float32)
    opening = (docs == docs[0]).astype(jnp.float32)
    stacked = (
        x_wide.transpose(1, 0, 2, 3),
        b_split.transpose(1, 0, 2),
        c_split.transpose(1, 0, 2),
        logs.reshape(length, groups, per_group).transpose(1, 0, 2),
        dt.reshape(length, groups, per_group).transpose(1, 0, 2),
    )
    inner, end_state = lax.map(lambda item: group_terms(item, causal, ending), stacked)
    end_state = end_state.reshape(heads, HEAD_DIM, STATE)
    whole_decay = jnp.exp(logs[length - 1]) * (docs[0] == docs[length - 1]).astype(jnp.float32)
    element = (docs[:1], docs[length - 1 :], whole_decay, end_state)
    identity = (
        jnp.full((1,), -1, jnp.int32),
        jnp.full((1,), -1, jnp.int32),
        jnp.ones((heads,), jnp.float32),
        jnp.zeros_like(end_state),
    )
    _, prior_last, _, incoming = entering(element, "ctx", combine_states, identity)
    linked = (prior_last == docs[:1]).astype(jnp.float32)
    reach = jnp.exp(logs) * opening[:, None] * linked
    outer = jnp.einsum(
        "tgn,ghpn->tghp",
        c_split.astype(jnp.float32),
        incoming.reshape(groups, per_group, HEAD_DIM, STATE),
        precision=lax.Precision.HIGHEST,
    )
    outer = outer * reach.reshape(length, groups, per_group)[:, :, :, None]
    inner = inner.transpose(1, 0, 2, 3)
    scan = (inner + outer).reshape(length, heads, HEAD_DIM) + skip[None, :, None] * x_wide.reshape(
        length, heads, HEAD_DIM
    )
    scan = scan.reshape(length, heads * HEAD_DIM)
    gated = scan * silu(gate_channels.astype(jnp.float32))
    grouped = gated.reshape(length, -1, HEADS * HEAD_DIM // GROUPS)
    grouped = grouped / jnp.sqrt(jnp.mean(grouped * grouped, axis=2, keepdims=True) + EPS)
    normed_scan = (grouped.reshape(length, -1) * norm_gain).astype(jnp.bfloat16)
    partial_value = jnp.dot(
        normed_scan,
        lax.all_gather(w_out, "ctx", axis=1, tiled=True),
        preferred_element_type=jnp.float32,
    )
    mixed = lax.psum_scatter(
        partial_value.astype(jnp.bfloat16), "head", scatter_dimension=0, tiled=True
    )
    ctx_count, head_count = (lax.axis_size("ctx"), lax.axis_size("head"))
    experts_all = ctx_count * head_count
    rows_all = residual.shape[0] * experts_all
    rows_sent = experts_all * slots_of(residual.shape[0], experts.shape[1], experts_all)
    if ctx_count % 2 == 0 and head_count == 2 and rows_all <= 2 * rows_sent:
        return moe_by_sums(mixed, residual, moe_gain, experts, gates, w_up, w_down)
    return moe_by_rows(mixed, residual, moe_gain, experts, gates, w_up, w_down)


def solution(mesh):
    return jax.shard_map(
        local,
        mesh=mesh,
        in_specs=(
            P(("parts", "ctx"), "head"),
            P(("parts", "ctx"), "head"),
            P(("parts", "ctx"), "head"),
            P(("parts", "ctx"), "head"),
            P(("parts", "ctx"), "head"),
            P("head"),
            P("head"),
            P("head"),
            P(("parts", "ctx")),
            P("head", "ctx"),
            P(("parts", "ctx", "head"), None),
            P(),
            P(("parts", "ctx", "head"), None),
            P(("parts", "ctx", "head"), None),
            P(("ctx", "head"), None, None),
            P(("ctx", "head"), None, None),
        ),
        out_specs=P(("parts", "ctx", "head"), None),
        check_vma=False,
    )
```

```python
import functools

import jax
import jax.numpy as jnp
from jax import lax
from jax.experimental import pallas as pl
from jax.experimental.pallas import tpu as pltpu
from jax.sharding import PartitionSpec as P

HEAD_DIM = 64
STATE = 128


EPS = 1e-05


def expert_rows(received, up_weight, down_weight):
    sources, items, width = received.shape
    rows = received.reshape(sources * items, width)
    up = jnp.dot(rows, up_weight, preferred_element_type=jnp.float32)
    act = jnp.square(jnp.maximum(up, 0.0)).astype(jnp.bfloat16)
    result = jnp.dot(act, down_weight, preferred_element_type=jnp.float32).astype(jnp.bfloat16)
    return result.reshape(sources, items, width)


LANES = 128


def dot(left, right, left_dim, right_dim):
    return lax.dot_general(
        left,
        right,
        (((left_dim,), (right_dim,)), ((), ())),
        preferred_element_type=jnp.float32,
    )


def whole_spec():
    return pl.BlockSpec(memory_space=pltpu.VMEM)


def scalar_spec():
    return pl.BlockSpec(memory_space=pltpu.SMEM)


def call(kernel, outs, specs, cost, limit, name):
    return pl.pallas_call(
        kernel,
        in_specs=specs,
        out_specs=[whole_spec() for _ in outs],
        out_shape=outs,
        compiler_params=pltpu.CompilerParams(vmem_limit_bytes=limit << 20),
        cost_estimate=pl.CostEstimate(flops=cost[0], bytes_accessed=cost[1], transcendentals=0),
        name=name,
    )


def shaped(shape, dtype):
    return jax.ShapeDtypeStruct(shape, dtype)


def three_pieces(value):
    first = value.astype(jnp.bfloat16)
    rest = value - first.astype(jnp.float32)
    second = rest.astype(jnp.bfloat16)
    third = (rest - second.astype(jnp.float32)).astype(jnp.bfloat16)
    return (first, second, third)


def packed_width(experts_all):
    return -(-3 * experts_all // LANES) * LANES


def moe_rows_kernel(experts_all, mixed, residual, gain, experts, gates, hidden_out, packed_out):
    rows, width = residual.shape
    hidden = (residual[...].astype(jnp.float32) + mixed[...].astype(jnp.float32)).astype(jnp.bfloat16)
    hidden_out[...] = hidden
    wide = hidden.astype(jnp.float32)
    scale = jnp.sqrt(jnp.mean(wide * wide, axis=1, keepdims=True) + EPS)
    packed_out[:, :width] = (wide / scale * gain[...]).astype(jnp.bfloat16)
    lanes = packed_out.shape[1] - width
    lane = lax.broadcasted_iota(jnp.int32, (rows, lanes), 1)
    table = jnp.zeros((rows, lanes), jnp.float32)
    for k in range(experts.shape[1]):
        chosen = experts[:, k : k + 1]
        hit = (lane == chosen) | (lane == chosen + experts_all) | (lane == chosen + 2 * experts_all)
        table = table + jnp.where(hit, gates[:, k : k + 1], 0.0)
    first, second, third = three_pieces(table)
    picked = jnp.where(lane < experts_all, first, jnp.where(lane < 2 * experts_all, second, third))
    packed_out[:, width:] = picked


def expert_pair_kernel(experts_all, ids, near, far, up0, down0, up1, down1, near_out, far_out):
    rows = near.shape[0]
    width = near_out.shape[1]
    x = jnp.concatenate([near[:, :width], far[:, :width]], axis=0)
    table = jnp.concatenate([near[:, width:], far[:, width:]], axis=0).astype(jnp.float32)
    lane = lax.broadcasted_iota(jnp.int32, table.shape, 1)
    acts, weights = ([], [])
    for k, up in enumerate((up0, up1)):
        value = dot(x, up[...], 1, 1)
        acts.append(jnp.square(jnp.maximum(value, 0.0)).astype(jnp.bfloat16))
        mine = ids[k]
        hit = (lane == mine) | (lane == mine + experts_all) | (lane == mine + 2 * experts_all)
        weights.append(jnp.sum(jnp.where(hit, table, 0.0), axis=1, keepdims=True))
    step = width
    for part in (3, 2):
        if width % (part * LANES) == 0:
            step = width // part
            break
    for at in range(0, width, step):
        piece = pl.ds(at, step)
        result = dot(acts[0], down0[:, piece], 1, 0) * weights[0] + dot(acts[1], down1[:, piece], 1, 0) * weights[1]
        near_out[:, piece] = result[:rows].astype(near_out.dtype)
        far_out[:, piece] = result[rows:].astype(far_out.dtype)


def moe_by_sums(mixed, residual, moe_gain, experts, gates, w_up, w_down):
    rows, width = residual.shape
    units = w_down.shape[1]
    ctx_count, head_count = (lax.axis_size("ctx"), lax.axis_size("head"))
    experts_all = ctx_count * head_count
    high = ctx_count // 2
    ring = [(z * 2 + y, (z + 1) % high * 2 + y) for z in range(high) for y in range(2)]
    across = [(z * 2 + y, z * 2 + 1 - y) for z in range(high) for y in range(2)]
    swap = [(0, 1), (1, 0)]
    up_own = jnp.swapaxes(w_up[0], 0, 1)
    down_own = w_down[0]
    up_other = lax.ppermute(up_own, "head", swap)
    down_other = lax.ppermute(down_own, "head", swap)
    mine = lax.axis_index("ctx") * head_count + lax.axis_index("head")
    other = lax.axis_index("ctx") * head_count + 1 - lax.axis_index("head")
    ids = jnp.stack([mine, other]).astype(jnp.int32)
    extra = packed_width(experts_all)
    hidden, packed = call(
        functools.partial(moe_rows_kernel, experts_all),
        [shaped((rows, width), jnp.bfloat16), shaped((rows, width + extra), jnp.bfloat16)],
        [whole_spec()] * 5,
        (10 * rows * width, 8 * rows * width),
        8,
        "moe_rows",
    )(mixed, residual, moe_gain.reshape(1, width), experts, gates)
    near = [packed]
    for _ in range(1, high):
        near.append(lax.ppermute(near[-1], "ctx", ring))
    far = [lax.ppermute(value, "ctx", across) for value in near]
    partials = []
    for r in range(high):
        partials.append(
            call(
                functools.partial(expert_pair_kernel, experts_all),
                [shaped((rows, width), jnp.bfloat16)] * 2,
                [scalar_spec()] + [whole_spec()] * 6,
                (16 * rows * width * units, 8 * width * units),
                26,
                "expert_pair",
            )(ids, near[r], far[r], up_own, down_own, up_other, down_other)
        )
    sums = [
        own.astype(jnp.float32) + lax.ppermute(away, "ctx", across).astype(jnp.float32)
        for own, away in partials
    ]
    total = None
    for r in list(range(1, high)) + [0]:
        value = sums[r] if total is None else sums[r] + total.astype(jnp.float32)
        if r == 0:
            return (hidden.astype(jnp.float32) + value).astype(jnp.bfloat16)
        total = lax.ppermute(value.astype(jnp.bfloat16), "ctx", ring)


def slots_of(rows, top, experts_all):
    return min(rows, max(4, 3 * rows * top // (2 * experts_all)))


def moe_by_rows(mixed, residual, moe_gain, experts, gates, w_up, w_down):
    mamba_out = mixed.astype(jnp.float32)
    hidden = (residual.astype(jnp.float32) + mamba_out).astype(jnp.bfloat16)
    widened = hidden.astype(jnp.float32)
    moe_in = (
        widened / jnp.sqrt(jnp.mean(widened * widened, axis=1, keepdims=True) + EPS) * moe_gain
    ).astype(jnp.bfloat16)
    rows_dev = moe_in.shape[0]
    top = experts.shape[1]
    width = moe_in.shape[1]
    ctx_count = lax.axis_size("ctx")
    head_count = lax.axis_size("head")
    experts_all = ctx_count * head_count
    capacity = slots_of(rows_dev, top, experts_all)
    picks = experts.reshape(-1)
    pick_index = jnp.arange(picks.shape[0], dtype=jnp.int32)
    earlier = (picks[:, None] == picks[None, :]) & (pick_index[None, :] < pick_index[:, None])
    slot = jnp.sum(earlier.astype(jnp.int32), axis=1)
    target = (picks * capacity + slot).reshape(rows_dev, top)
    places = jnp.arange(experts_all * capacity, dtype=jnp.int32)
    routing = jnp.any(target[None, :, :] == places[:, None, None], axis=2).astype(jnp.bfloat16)
    outgoing = jnp.dot(routing, moe_in, preferred_element_type=jnp.float32).astype(jnp.bfloat16)
    outgoing = outgoing.reshape(experts_all, capacity, width)
    up_weight = w_up[0]
    down_weight = w_down[0]
    results = expert_rows(
        lax.all_to_all(outgoing, ("ctx", "head"), split_axis=0, concat_axis=0, tiled=True),
        up_weight,
        down_weight,
    )
    returned = lax.all_to_all(results, ("ctx", "head"), split_axis=0, concat_axis=0, tiled=True)
    flat_back = returned.reshape(experts_all * capacity, width)
    chosen = flat_back[target].astype(jnp.float32)
    mixture = jnp.sum(chosen * gates[:, :, None], axis=1)
    return (widened + mixture).astype(jnp.bfloat16)


TAIL_ROWS = 8
FAR_BELOW = -1e30


def exact_dot(left, right, left_dim, right_dim):
    return lax.dot_general(
        left,
        right,
        (((left_dim,), (right_dim,)), ((), ())),
        precision=lax.Precision.HIGHEST,
        preferred_element_type=jnp.float32,
    )


def tail_block(decay, last):
    row = lax.broadcasted_iota(jnp.int32, (TAIL_ROWS, decay.shape[1]), 0)
    first, second, third = (piece.astype(jnp.float32) for piece in three_pieces(decay))
    block = jnp.where(row == 0, first, jnp.where(row == 1, second, third))
    block = jnp.where(row == 3, last, block)
    return jnp.where(row > 3, 0.0, block).astype(jnp.bfloat16)


def read_tail(message):
    tail = message[message.shape[0] - TAIL_ROWS :, :].astype(jnp.float32)
    return (tail[0:1] + tail[1:2] + tail[2:3], tail[3:4])


def scan_kernel(x_ref, b_ref, c_ref, dt_ref, rates, skip, docs_down, docs_along, inner_out, reach_out, message_out):
    length, channels = x_ref.shape
    heads = dt_ref.shape[0]
    groups = b_ref.shape[1] // STATE
    span = channels // groups
    per_group = heads // groups
    down = lax.broadcasted_iota(jnp.int32, (length, length), 0)
    along = lax.broadcasted_iota(jnp.int32, (length, length), 1)
    causal = (down >= along).astype(jnp.float32)
    same = (down == along).astype(jnp.float32)
    mask = (docs_down[...] == docs_along[...]) & (down >= along)
    dt = dt_ref[...]
    steps = -rates[...] * dt
    logs = exact_dot(causal, steps, 1, 1)
    logs_along = exact_dot(steps, causal, 1, 1)
    dt_down = exact_dot(same, dt, 1, 1)
    last = docs_down[length - 1 : length, :]
    ending = (docs_down[...] == last).astype(jnp.float32)
    opening = (docs_down[...] == docs_down[0:1, :]).astype(jnp.float32)
    end = logs[length - 1 : length, :]
    tail = jnp.exp(end - logs) * ending * dt_down
    reach = jnp.exp(logs) * opening
    spread = (
        lax.broadcasted_iota(jnp.int32, (heads, channels), 1) // HEAD_DIM
        == lax.broadcasted_iota(jnp.int32, (heads, channels), 0)
    ).astype(jnp.float32)
    reach_out[...] = exact_dot(reach, spread, 1, 0)
    rows = jnp.concatenate([jnp.exp(end), skip[...], jnp.zeros((6, heads), jnp.float32)], axis=0)
    wide_rows = exact_dot(rows, spread, 1, 0)
    decay, direct = (wide_rows[0:1], wide_rows[1:2])
    x_all = x_ref[...]
    x_wide = x_all.astype(jnp.float32)
    ended = (x_wide * exact_dot(tail, spread, 1, 0)).astype(jnp.bfloat16)
    lane = lax.broadcasted_iota(jnp.int32, (length, 2 * HEAD_DIM), 1)
    for g in range(groups):
        b_group = b_ref[:, g * STATE : (g + 1) * STATE]
        c_group = c_ref[:, g * STATE : (g + 1) * STATE]
        scores = dot(c_group, b_group, 1, 1)
        for pair in range(per_group // 2):
            at = g * span + pair * 2 * HEAD_DIM
            x_pair = x_all[:, at : at + 2 * HEAD_DIM]
            results = []
            for h in (g * per_group + 2 * pair, g * per_group + 2 * pair + 1):
                gap = logs[:, h : h + 1] - logs_along[h : h + 1, :]
                weight = jnp.exp(jnp.where(mask, gap, FAR_BELOW)) * (scores * dt[h : h + 1, :])
                results.append(dot(weight.astype(jnp.bfloat16), x_pair, 1, 0))
            both = jnp.where(lane < HEAD_DIM, results[0], results[1])
            inner_out[:, at : at + 2 * HEAD_DIM] = (
                both + direct[:, at : at + 2 * HEAD_DIM] * x_wide[:, at : at + 2 * HEAD_DIM]
            )
        state = dot(b_group, ended[:, g * span : (g + 1) * span], 0, 0)
        message_out[:STATE, g * span : (g + 1) * span] = state.astype(jnp.bfloat16)
    message_out[STATE:, :] = tail_block(decay, last.astype(jnp.float32))


def link_states(near, far):
    near_decay, near_last = read_tail(near)
    far_decay, far_last = read_tail(far)
    factor = near_decay * (near_last == far_last).astype(jnp.float32)
    state = near[:STATE, :].astype(jnp.float32) + factor * far[:STATE, :].astype(jnp.float32)
    return (state, near_decay * far_decay, near_last)


def link_kernel(near_ref, far_ref, out):
    state, decay, last = link_states(near_ref[...], far_ref[...])
    out[:STATE, :] = state.astype(jnp.bfloat16)
    out[STATE:, :] = tail_block(decay, last)


def gate_kernel(near_ref, far_ref, c_ref, inner, reach, gate, gain, docs_down, out):
    length, channels = inner.shape
    groups = c_ref.shape[1] // STATE
    span = channels // groups
    state, _, last = link_states(near_ref[...], far_ref[...])
    state = (state * (last == docs_down[0:1, :].astype(jnp.float32)).astype(jnp.float32)).astype(jnp.bfloat16)
    for g in range(groups):
        piece = slice(g * span, (g + 1) * span)
        outer = dot(c_ref[:, g * STATE : (g + 1) * STATE], state[:, piece], 1, 0)
        scan = inner[:, piece] + outer * reach[:, piece]
        value = gate[:, piece].astype(jnp.float32)
        gated = scan * (value / (1.0 + jnp.exp(-value)))
        scale = jnp.sqrt(jnp.mean(gated * gated, axis=1, keepdims=True) + EPS)
        out[:, piece] = (gated / scale * gain[:, piece]).astype(jnp.bfloat16)


def normed_scan(channels, gate_channels, bmat, cmat, dt, rates, skip, norm_gain, docs):
    length, width = channels.shape
    heads = dt.shape[1]
    docs_down = docs.reshape(length, 1)
    inner, reach, message = call(
        scan_kernel,
        [
            shaped((length, width), jnp.float32),
            shaped((length, width), jnp.float32),
            shaped((STATE + TAIL_ROWS, width), jnp.bfloat16),
        ],
        [whole_spec()] * 8,
        (6 * length * length * width, 16 * length * width),
        16,
        "scan_local",
    )(
        channels,
        bmat,
        cmat,
        jnp.swapaxes(dt, 0, 1),
        rates.reshape(heads, 1),
        skip.reshape(1, heads),
        docs_down,
        docs.reshape(1, length),
    )
    count = lax.axis_size("ctx")

    def shifted(value, by):
        return lax.ppermute(value, "ctx", [(i, i + by) for i in range(count - by)])

    near = shifted(message, 1)
    far = shifted(message, 2)
    reached = 2
    while 2 * reached <= count // 2:
        near = call(
            link_kernel,
            [shaped(message.shape, jnp.bfloat16)],
            [whole_spec()] * 2,
            (4 * STATE * width, 6 * STATE * width),
            8,
            "scan_link",
        )(near, far)[0]
        far = shifted(near, reached)
        reached *= 2
    return call(
        gate_kernel,
        [shaped((length, width), jnp.bfloat16)],
        [whole_spec()] * 8,
        (2 * length * STATE * width, 20 * length * width),
        16,
        "scan_gate",
    )(near, far, cmat, inner, reach, gate_channels, norm_gain.reshape(1, width), docs_down)[0]


def local(
    channels,
    gate_channels,
    bmat,
    cmat,
    dt,
    rates,
    skip,
    norm_gain,
    docs,
    w_out,
    residual,
    moe_gain,
    experts,
    gates,
    w_up,
    w_down,
):
    normed = normed_scan(channels, gate_channels, bmat, cmat, dt, rates, skip, norm_gain, docs)
    partial_value = jnp.dot(
        normed,
        lax.all_gather(w_out, "ctx", axis=1, tiled=True),
        preferred_element_type=jnp.float32,
    )
    mixed = lax.psum_scatter(
        partial_value.astype(jnp.bfloat16), "head", scatter_dimension=0, tiled=True
    )
    ctx_count, head_count = (lax.axis_size("ctx"), lax.axis_size("head"))
    experts_all = ctx_count * head_count
    rows_all = residual.shape[0] * experts_all
    rows_sent = experts_all * slots_of(residual.shape[0], experts.shape[1], experts_all)
    if ctx_count % 2 == 0 and head_count == 2 and rows_all <= 2 * rows_sent:
        return moe_by_sums(mixed, residual, moe_gain, experts, gates, w_up, w_down)
    return moe_by_rows(mixed, residual, moe_gain, experts, gates, w_up, w_down)


def solution(mesh):
    return jax.shard_map(
        local,
        mesh=mesh,
        in_specs=(
            P(("parts", "ctx"), "head"),
            P(("parts", "ctx"), "head"),
            P(("parts", "ctx"), "head"),
            P(("parts", "ctx"), "head"),
            P(("parts", "ctx"), "head"),
            P("head"),
            P("head"),
            P("head"),
            P(("parts", "ctx")),
            P("head", "ctx"),
            P(("parts", "ctx", "head"), None),
            P(),
            P(("parts", "ctx", "head"), None),
            P(("parts", "ctx", "head"), None),
            P(("ctx", "head"), None, None),
            P(("ctx", "head"), None, None),
        ),
        out_specs=P(("parts", "ctx", "head"), None),
        check_vma=False,
    )
```
